512 devices in a mesh: section: 16 (over x_lo, z), dp: 32 (over x_hi, y, core).
Axes of the slice: x: 4 (x_hi: 2, x_lo: 2; x = x_hi * 2 + x_lo), y: 8, z: 8, core: 2. Of those that a mesh axis runs over, the one named last changes fastest.
Arguments:
- act_in: float32 [16, 2, 32, 15, 15, 256], P('section', None, 'dp'), may hold values from -6 to 6
- act_mid: float32 [16, 2, 32, 15, 15, 256], P('section', None, 'dp'), may hold values from 0 to 2
- relu_mask: int32 [16, 2, 32, 15, 15, 256], P('section', None, 'dp'), may hold values 0 or 1
- arriving: float32 [16, 32, 15, 15, 256], P('section', 'dp'), may hold values from -6 to 6
- loss_grad: float32 [1, 32, 15, 15, 256], P(None, 'dp'), may hold values from -6 to 6
- w_first: float32 [16, 1792, 256], P('section', 'dp'), may hold values from -0.125 to 0.125
- w_second: float32 [16, 1792, 256], P('section', 'dp'), may hold values from -0.125 to 0.125
Outputs:
- data_grad: float32 [16, 2, 32, 15, 15, 256], P('section', None, 'dp')
- first_grad: float32 [16, 1792, 256], P('section', 'dp')
- second_grad: float32 [16, 1792, 256], P('section', 'dp')
The draws below stay inside these ranges and needn't reach their ends.
All inputs are finite; a program needn't handle non-finite values. No bound on the sum of `relu_mask` on one device may be relied on, other than what follows from the above.
Results may differ from the reference program's by a relative error of at most 0.00011.
Values sent between devices are 32-bit elements; how exact they have to be, the bound alone decides.
A program may use at most 64 MiB of HBM per device.

```python
import jax
import jax.numpy as jnp
from jax import lax

C = 256
HGT = 15
WID = 15
TICKS = 2
SECTIONS = 16
IMAGES = 32


def plant(entries, stream_key, low, high):
    longest = entries.shape.index(max(entries.shape))
    spots = []
    for shift in (0, 1):
        where = [jax.random.randint(jax.random.fold_in(stream_key, axis), (), 0, length) for axis, length in enumerate(entries.shape)]
        where[longest] = (where[longest] + shift) % entries.shape[longest]
        spots.append(tuple(where))
    return entries.at[spots[0]].set(low).at[spots[1]].set(high)


def spiked(drawn, own_key, source, target, blocks, factor):
    def block_of(position):
        return (jnp.arange(drawn.shape[position]) // (drawn.shape[position] // blocks)).reshape((-1,) + (1,) * (drawn.ndim - 1 - position))

    one_side = jax.random.permutation(own_key, blocks)[block_of(target)]
    other_side = (block_of(target) + blocks // 2) % blocks
    return jnp.where((block_of(source) == one_side) | (block_of(source) == other_side), factor * drawn, drawn)


def block_levels(rng, shape, shards, low, largest):
    def one(dim, shards_of):
        draws = jax.random.uniform(jax.random.fold_in(jax.random.fold_in(rng, 6), dim), (shards_of,), jnp.float32, low / len(shards), largest / len(shards))
        return jnp.repeat(jnp.exp(draws), shape[dim] // shards_of).reshape((-1,) + (1,) * (len(shape) - dim - 1))

    gain = one(*shards[0])
    for cut in shards[1:]:
        gain = gain * one(*cut)
    return gain


def normal_values(key, shape, width, bound, split=(), kind=jnp.bfloat16):
    array = jax.random.normal(key, shape, jnp.float32) * width
    if len(split) > 0:
        array = block_levels(key, shape, split, -0.22, 0.18) * array
    return jnp.clip(array, min=-bound, max=bound).astype(kind)


def bell_draw_with(stream_key, shape, deviation, limit, cuts, heavy, kind=jnp.bfloat16):
    array = deviation * jax.random.normal(stream_key, shape, jnp.float32)
    if cuts:
        array = array * block_levels(stream_key, shape, cuts, -0.22, 0.18)
    return jnp.clip(spiked(array, jax.random.fold_in(stream_key, 3), *heavy), -limit, limit).astype(kind)


def setup_inputs(seed: int = 0) -> dict:
    splits = jax.random.split(jax.random.key(seed), 8)
    act_in = bell_draw_with(splits[0], (SECTIONS, TICKS, IMAGES, HGT, WID, C), 1.0, 6.0, ((0, 16), (2, 32)), (2, 5, 32, 2.75), jnp.float32)
    act_mid = jnp.clip(2.0 * jax.random.uniform(splits[1], (SECTIONS, TICKS, IMAGES, HGT, WID, C), jnp.float32) ** block_levels(splits[1], (SECTIONS, TICKS, IMAGES, HGT, WID, C), ((0, 16), (2, 32)), -0.2, 0.2), 0.0, 2.0)
    relu_mask = plant((jax.random.randint(splits[2], (SECTIONS, TICKS, IMAGES, HGT, WID, C), 0, 2) < 1).astype(jnp.int32), jax.random.fold_in(splits[2], 1), 0, 1)
    arriving = normal_values(splits[3], (SECTIONS, IMAGES, HGT, WID, C), 1.0, 6.0, ((0, 16), (1, 32)), jnp.float32)
    loss_grad = normal_values(splits[4], (TICKS - 1, IMAGES, HGT, WID, C), 1.0, 6.0, ((1, 32),), jnp.float32)
    w_first = normal_values(splits[5], (SECTIONS, 7 * C, C), (7 * C) ** -0.5, 0.125, ((0, 16), (1, 32)), jnp.float32)
    w_second = normal_values(splits[6], (SECTIONS, 7 * C, C), (7 * C) ** -0.5, 0.125, ((0, 16), (1, 32)), jnp.float32)
    return dict(act_in=act_in, act_mid=act_mid, relu_mask=relu_mask, arriving=arriving, loss_grad=loss_grad, w_first=w_first, w_second=w_second)


def spread_taps(values, spatial):
    widths = [(0, 0)] * 4
    widths[spatial] = (3, 3)
    padded = jnp.pad(values, widths)
    extent = values.shape[spatial]
    pieces = [lax.slice_in_dim(padded, offset, offset + extent, axis=spatial) for offset in range(7)]
    return jnp.concatenate(pieces, axis=-1)


def fold_taps(products, spatial):
    channels = products.shape[-1] // 7
    widths = [(0, 0)] * 4
    widths[spatial] = (3, 3)
    padded = jnp.pad(products, widths)
    extent = products.shape[spatial]
    summed = jnp.zeros(products.shape[:-1] + (channels,), products.dtype)
    for offset in range(7):
        window = lax.slice_in_dim(padded, 6 - offset, 6 - offset + extent, axis=spatial)
        summed = summed + window[..., offset * channels:(offset + 1) * channels]
    return summed


def project_taps(values, weight):
    return jnp.einsum("nhwc,kc->nhwk", values, weight, precision=lax.Precision.HIGHEST)


def section_backward(incoming, relu_mask, w_first, w_second):
    mid_grad = fold_taps(project_taps(incoming, w_second), 1)
    pre_grad = mid_grad * relu_mask.astype(jnp.float32)
    data_grad = fold_taps(project_taps(pre_grad, w_first), 2)
    return data_grad, pre_grad


def replica_sum(activations, grad_rows, spatial, mean_scale):
    tick_count, images = activations.shape[:2]
    patches = spread_taps(activations.reshape((tick_count * images,) + activations.shape[2:]), spatial)
    grouped = grad_rows.reshape((tick_count * images,) + grad_rows.shape[2:])
    return jnp.einsum("nhwk,nhwc->kc", patches, grouped, precision=lax.Precision.HIGHEST) * mean_scale


def reference(act_in, act_mid, relu_mask, arriving, loss_grad, w_first, w_second):
    tick_count = act_in.shape[1]
    incoming = arriving
    in_list, pre_list, out_list = [], [], []
    for tick_index in range(tick_count):
        if tick_index > 0:
            incoming = jnp.concatenate([out_list[-1][1:], loss_grad[tick_index - 1][None]], axis=0)
        outgoing, pre_grad = lax.map(lambda packed: section_backward(*packed),
                                     (incoming, relu_mask[:, tick_index], w_first, w_second))
        in_list.append(incoming)
        pre_list.append(pre_grad)
        out_list.append(outgoing)
    data_grad = jnp.stack(out_list, axis=1)
    incoming_all = jnp.stack(in_list, axis=1)
    pre_all = jnp.stack(pre_list, axis=1)
    mean_scale = 1.0 / (tick_count * act_in.shape[2])

    def filter_grads(packed):
        inputs_section, mids_section, incoming_section, pre_section = packed
        first_part = replica_sum(inputs_section, pre_section, 2, mean_scale)
        second_part = replica_sum(mids_section, incoming_section, 1, mean_scale)
        return first_part, second_part

    first_grad, second_grad = lax.map(filter_grads, (act_in, act_mid, incoming_all, pre_all))
    return data_grad, first_grad, second_grad
```

```python
import functools

import jax
import jax.numpy as jnp
from jax import lax
from jax.experimental import pallas as pl
from jax.experimental.pallas import tpu as pltpu
from jax.sharding import PartitionSpec as P

MESH = pl.DeviceIdType.MESH
F32, BF16 = jnp.float32, jnp.bfloat16
PITCH = 16


def split(value):
    high = value.astype(BF16)
    return high, (value - high.astype(F32)).astype(BF16)


def dot_nt(a, b):
    return lax.dot_general(a, b, (((1,), (1,)), ((), ())), preferred_element_type=F32)


def dot_nn(a, b):
    return lax.dot_general(a, b, (((1,), (0,)), ((), ())), preferred_element_type=F32)


def kernel(
    sections,
    replicas,
    act_in,
    act_mid,
    relu_mask,
    arriving,
    loss_grad,
    w_first,
    w_second,
    data_grad,
    first_grad,
    second_grad,
    acts,
    masks,
    ups,
    act_t,
    rows_hi,
    rows_lo,
    cols_hi,
    cols_lo,
    weights,
    w_hi,
    w_lo,
    total,
    passed,
    above,
    out_map,
    grads,
    pair_in,
    ring_in,
    cross_in,
    grad_out,
    load_sem,
    own_sem,
    gather_send,
    gather_ring,
    gather_pair,
    shift_sem,
    reduce_send,
    reduce_pair,
    reduce_ring,
    reduce_cross,
    store_sem,
):
    ny = replicas // 4
    half = ny // 2
    shard, chans = w_first.shape[1:]
    height, width = act_in.shape[3:5]
    rows = height * PITCH
    taps = 7
    sec = lax.axis_index("section")
    dp = lax.axis_index("dp")
    x, y, c = dp // (2 * ny), (dp // 2) % ny, dp % 2

    def device(xr, rel, other):
        xx = 1 - x if xr else x
        cc = 1 - c if other else c
        return xx * (2 * ny) + lax.rem(y + rel + ny, ny) * 2 + cc

    def block(xr, rel, other=False):
        return pl.ds(pl.multiple_of(device(xr, rel, other) * shard, 8), shard)

    def slot(xr, rel):
        return xr * ny + rel % ny

    pair = {"dp": device(0, 0, True)}
    cross = {"dp": device(1, 0, False)}
    ahead = {1: {"dp": device(0, 1, False)}, -1: {"dp": device(0, -1, False)}}
    prev_section = {"section": lax.rem(sec + sections - 1, sections)}
    next_section = {"section": lax.rem(sec + 1, sections)}

    loads = []
    for t in range(2):
        loads.append((arriving.at[0, 0] if t == 0 else loss_grad.at[0, 0], ups.at[t]))
    for t in range(2):
        loads.append((act_mid.at[0, t, 0], acts.at[0, t]))
    for t in range(2):
        loads.append((relu_mask.at[0, t, 0], masks.at[t]))
    for t in range(2):
        loads.append((act_in.at[0, t, 0], acts.at[1, t]))
    loads = [pltpu.make_async_copy(s, d, load_sem.at[i]) for i, (s, d) in enumerate(loads)]
    for copy in loads:
        copy.start()
    shards = (w_second.at[0], w_first.at[0])
    own = [
        pltpu.make_async_copy(shards[w], weights.at[w, block(0, 0)], own_sem.at[w])
        for w in range(2)
    ]
    for copy in own:
        copy.start()

    barrier = pltpu.get_barrier_semaphore()
    friends = (pair, cross, ahead[1], ahead[-1], prev_section, next_section)
    for friend in friends:
        pl.semaphore_signal(barrier, inc=1, device_id=friend, device_id_type=MESH)
    pl.semaphore_wait(barrier, len(friends))

    def gather_copy(w, src, xr, rel, other, sem, to):
        return pltpu.make_async_remote_copy(
            src_ref=src,
            dst_ref=weights.at[w, block(xr, rel, other)],
            send_sem=gather_send.at[w],
            recv_sem=sem,
            device_id=to,
            device_id_type=MESH,
        )

    def gather_start(w):
        src = shards[w]
        for way in (1, -1):
            gather_copy(w, src, 0, 0, False, gather_ring.at[w, slot(0, -way)], ahead[way]).start()
        gather_copy(w, src, 0, 0, False, gather_ring.at[w, slot(1, 0)], cross).start()
        gather_copy(w, src, 0, 0, False, gather_pair.at[w, slot(0, 0)], pair).start()

    def gather_arrival(w, way, xr, hop):
        rel = -way * hop
        here = weights.at[w, block(xr, rel)]
        gather_copy(w, here, xr, rel, False, gather_ring.at[w, slot(xr, rel)], cross).wait_recv()
        ways = (1, -1) if hop == 0 else (way,)
        for onward in ways:
            last = hop + 1 == half
            if hop + 1 < half or (last and xr == (0 if onward == 1 else 1)):
                sem = gather_ring.at[w, slot(xr, rel - onward)]
                gather_copy(w, here, xr, rel, False, sem, ahead[onward]).start()
        gather_copy(w, here, xr, rel, False, gather_pair.at[w, slot(xr, rel)], pair).start()

    def gather_hop(hop):
        for xr in (0, 1):
            for w in range(2):
                if hop == 1 and xr == 1:
                    gather_arrival(w, 1, 1, 0)
            for w in range(2):
                for way in (1, -1):
                    if hop < half:
                        gather_arrival(w, way, xr, hop)

    def gather_end(w):
        gather_arrival(w, 1, 0, half)
        gather_arrival(w, -1, 1, half)

    def gather_pair_wait(w):
        own[w].wait()
        for xr in (0, 1):
            for rel in range(ny):
                here = weights.at[w, block(xr, rel, True)]
                sem = gather_pair.at[w, slot(xr, rel)]
                gather_copy(w, here, xr, rel, True, sem, pair).wait_recv()

    def round_weights(w):
        high, low = split(weights[w])
        w_hi[w] = high
        w_lo[w] = low

    top = 3 * PITCH

    def set_rows(t, value):
        high, low = split(value)
        rows_hi[t, top : top + rows] = high
        rows_lo[t, top : top + rows] = low

    def row_tap(t, k, count):
        at = slice((6 - k) * PITCH, (6 - k) * PITCH + count)
        return rows_hi[t, at], rows_lo[t, at]

    def padded(value):
        return jnp.concatenate(
            [value, jnp.zeros((height, PITCH - width, chans), value.dtype)], axis=1
        ).reshape(rows, chans)

    def transpose_acts(which, t):
        value = padded(acts[which, t])
        value = jnp.concatenate([value, jnp.zeros((256 - rows, chans), F32)], axis=0)
        high, low = split(value.T)
        act_t[which, t, 0] = high
        act_t[which, t, 1] = low

    def project(lhs, w):
        for k in range(taps):
            at = pl.ds(k * chans, chans)
            high, low = lhs(k)
            part = (
                dot_nt(high, w_hi[w, at]) + dot_nt(high, w_lo[w, at]) + dot_nt(low, w_hi[w, at])
            )
            if k == 0:
                total[...] = part
            else:
                total[...] += part

    def correlate(w, t, rhs):
        which = w
        for k in range(taps):
            at = pl.ds(k * chans, chans)
            high, low = rhs(k)
            a_hi, a_lo = act_t[which, t, 0], act_t[which, t, 1]
            part = dot_nn(a_hi, high) + dot_nn(a_hi, low) + dot_nn(a_lo, high)
            if t == 0:
                grads[w, at] = part
            else:
                grads[w, at] += part

    def set_cols(t):
        pre = total[...] * padded(masks[t]).astype(F32)
        column = lax.broadcasted_iota(jnp.int32, (rows, chans), 0) % PITCH
        for k in range(taps):
            by = k - 3
            moved = pre if by == 0 else pltpu.roll(pre, by % rows, 0)
            inside = (column >= by) & (column < PITCH + by)
            high, low = split(jnp.where(inside, moved, 0.0))
            cols_hi[k, 0:rows] = high
            cols_lo[k, 0:rows] = low

    def col_tap(count):
        return lambda k: (cols_hi[k, 0:count], cols_lo[k, 0:count])

    def give_map(t):
        out_map[t] = total[...].reshape(height, PITCH, chans)[:, :width]
        copy = pltpu.make_async_copy(out_map.at[t], data_grad.at[0, t, 0], store_sem.at[t])
        copy.start()
        return copy

    def pair_copy(w, xr, rel):
        return pltpu.make_async_remote_copy(
            src_ref=grads.at[w, block(xr, rel, True)],
            dst_ref=pair_in.at[w, slot(xr, rel)],
            send_sem=reduce_send.at[w],
            recv_sem=reduce_pair.at[w, slot(xr, rel)],
            device_id=pair,
            device_id_type=MESH,
        )

    def ring_copy(w, way, xr, hop):
        rel = way * (half + 1 - hop)
        lane = 0 if way == 1 else 1
        return pltpu.make_async_remote_copy(
            src_ref=grads.at[w, block(xr, rel)],
            dst_ref=ring_in.at[w, lane, hop - 1, xr],
            send_sem=reduce_send.at[w],
            recv_sem=reduce_ring.at[w, lane, hop - 1, xr],
            device_id=ahead[way],
            device_id_type=MESH,
        )

    def cross_copy(w):
        return pltpu.make_async_remote_copy(
            src_ref=grads.at[w, block(1, 0)],
            dst_ref=cross_in.at[w],
            send_sem=reduce_send.at[w],
            recv_sem=reduce_cross.at[w],
            device_id=cross,
            device_id_type=MESH,
        )

    def pair_start(w):
        for dist in range(half, -1, -1):
            for rel in (dist,) if dist in (0, half) else (dist, -dist):
                for xr in (0, 1):
                    pair_copy(w, xr, rel).start()

    def came(way, xr, hop):
        return hop >= 1 and (hop > 1 or xr == (0 if way == 1 else 1))

    def ring_hop(w, hop):
        for xr in (0, 1):
            for way in (1, -1):
                if not came(way, xr, hop):
                    continue
                rel = way * (half + 1 - hop)
                pair_copy(w, xr, rel).wait_recv()
                here = block(xr, rel)
                value = grads[w, here] + pair_in[w, slot(xr, rel)]
                if came(way, xr, hop - 1):
                    ring_copy(w, way, xr, hop - 1).wait_recv()
                    value = value + ring_in[w, 0 if way == 1 else 1, hop - 2, xr]
                grads[w, here] = value
                ring_copy(w, way, xr, hop).start()

    def ring_end(w):
        for xr in (1, 0):
            pair_copy(w, xr, 0).wait_recv()
            here = block(xr, 0)
            value = grads[w, here] + pair_in[w, slot(xr, 0)]
            for way in (1, -1):
                ring_copy(w, way, xr, half).wait_recv()
                value = value + ring_in[w, 0 if way == 1 else 1, half - 1, xr]
            grads[w, here] = value
            if xr == 1:
                cross_copy(w).start()

    def give_grad(w):
        cross_copy(w).wait_recv()
        grad_out[w] = (grads[w, block(0, 0)] + cross_in[w]) * (1.0 / (2 * replicas))
        out = (second_grad, first_grad)[w].at[0]
        copy = pltpu.make_async_copy(grad_out.at[w], out, store_sem.at[2 + w])
        copy.start()
        return copy

    stores = []
    gather_start(0)
    gather_start(1)
    rows_hi[...] = jnp.zeros_like(rows_hi)
    rows_lo[...] = jnp.zeros_like(rows_lo)
    cols_hi[:, rows:256] = jnp.zeros((taps, 256 - rows, chans), BF16)
    cols_lo[:, rows:256] = jnp.zeros((taps, 256 - rows, chans), BF16)
    loads[0].wait()
    set_rows(0, padded(ups[0]))
    loads[2].wait()
    transpose_acts(0, 0)
    gather_hop(1)
    correlate(0, 0, lambda k: row_tap(0, k, 256))
    for hop in range(2, half):
        gather_hop(hop)
    loads[3].wait()
    transpose_acts(0, 1)
    loads[6].wait()
    transpose_acts(1, 0)
    loads[7].wait()
    transpose_acts(1, 1)
    gather_end(0)
    gather_end(1)
    gather_pair_wait(0)
    round_weights(0)
    project(lambda k: row_tap(0, k, rows), 0)
    loads[4].wait()
    set_cols(0)
    gather_pair_wait(1)
    round_weights(1)
    project(col_tap(rows), 1)
    passed[...] = total[...]
    shift = pltpu.make_async_remote_copy(
        src_ref=passed,
        dst_ref=above,
        send_sem=shift_sem.at[0],
        recv_sem=shift_sem.at[1],
        device_id=prev_section,
        device_id_type=MESH,
    )
    shift.start()
    stores.append(give_map(0))
    correlate(1, 0, col_tap(256))
    loads[1].wait()
    loads[5].wait()
    shift.wait_recv()
    is_last = jnp.full((rows, chans), sec, jnp.int32) == sections - 1
    set_rows(1, jnp.where(is_last, padded(ups[1]), above[...]))
    correlate(0, 1, lambda k: row_tap(1, k, 256))
    pair_start(0)
    project(lambda k: row_tap(1, k, rows), 0)
    ring_hop(0, 1)
    set_cols(1)
    correlate(1, 1, col_tap(256))
    pair_start(1)
    ring_hop(0, 2)
    ring_hop(1, 1)
    for hop in range(3, half + 1):
        ring_hop(0, hop)
        ring_hop(1, hop - 1)
    project(col_tap(rows), 1)
    stores.append(give_map(1))
    ring_hop(1, half)
    ring_end(0)
    ring_end(1)
    stores.append(give_grad(0))
    stores.append(give_grad(1))

    shift.wait_send()
    sent = pl.ds(0, (4 * ny - 1) * shard)
    for w in range(2):
        for buffer, sem in ((weights, gather_send), (grads, reduce_send)):
            pltpu.make_async_remote_copy(
                src_ref=buffer.at[w, sent],
                dst_ref=buffer.at[w, sent],
                send_sem=sem.at[w],
                recv_sem=sem.at[w],
                device_id=pair,
                device_id_type=MESH,
            ).wait_send()
    for copy in stores:
        copy.wait()


def local(sections, replicas, *args):
    act_in, w_first = args[0], args[5]
    height, width, chans = act_in.shape[3:]
    shard = w_first.shape[1]
    all_rows = shard * replicas
    ny = replicas // 4
    rows = height * PITCH
    dma = pltpu.SemaphoreType.DMA
    anywhere = pl.BlockSpec(memory_space=pl.ANY)
    scratch = [
        pltpu.VMEM((2, 2, height, width, chans), F32),
        pltpu.VMEM((2, height, width, chans), jnp.int32),
        pltpu.VMEM((2, height, width, chans), F32),
        pltpu.VMEM((2, 2, 2, chans, 256), BF16),
        pltpu.VMEM((2, 6 * PITCH + 256, chans), BF16),
        pltpu.VMEM((2, 6 * PITCH + 256, chans), BF16),
        pltpu.VMEM((7, 256, chans), BF16),
        pltpu.VMEM((7, 256, chans), BF16),
        pltpu.VMEM((2, all_rows, chans), F32),
        pltpu.VMEM((2, all_rows, chans), BF16),
        pltpu.VMEM((2, all_rows, chans), BF16),
        pltpu.VMEM((rows, chans), F32),
        pltpu.VMEM((rows, chans), F32),
        pltpu.VMEM((rows, chans), F32),
        pltpu.VMEM((2, height, width, chans), F32),
        pltpu.VMEM((2, all_rows, chans), F32),
        pltpu.VMEM((2, 2 * ny, shard, chans), F32),
        pltpu.VMEM((2, 2, ny // 2, 2, shard, chans), F32),
        pltpu.VMEM((2, shard, chans), F32),
        pltpu.VMEM((2, shard, chans), F32),
        dma((8,)),
        dma((2,)),
        dma((2,)),
        dma((2, 2 * ny)),
        dma((2, 2 * ny)),
        dma((2,)),
        dma((2,)),
        dma((2, 2 * ny)),
        dma((2, 2, ny // 2, 2)),
        dma((2,)),
        dma((4,)),
    ]
    return pl.pallas_call(
        functools.partial(kernel, sections, replicas),
        out_shape=(
            jax.ShapeDtypeStruct(act_in.shape, F32),
            jax.ShapeDtypeStruct(w_first.shape, F32),
            jax.ShapeDtypeStruct(w_first.shape, F32),
        ),
        in_specs=[anywhere] * 7,
        out_specs=(anywhere,) * 3,
        scratch_shapes=scratch,
        compiler_params=pltpu.CompilerParams(collective_id=0, has_side_effects=True),
    )(*args)


def solution(mesh):
    return jax.shard_map(
        functools.partial(local, mesh.shape["section"], mesh.shape["dp"]),
        mesh=mesh,
        in_specs=(
            P("section", None, "dp", None, None, None),
            P("section", None, "dp", None, None, None),
            P("section", None, "dp", None, None, None),
            P("section", "dp", None, None, None),
            P(None, "dp", None, None, None),
            P("section", "dp", None),
            P("section", "dp", None),
        ),
        out_specs=(
            P("section", None, "dp", None, None, None),
            P("section", "dp", None),
            P("section", "dp", None),
        ),
        check_vma=False,
    )
```

```python
import functools

import jax
import jax.numpy as jnp
from jax import lax
from jax.experimental import pallas as pl
from jax.experimental.pallas import tpu as pltpu
from jax.sharding import PartitionSpec as P

MESH = pl.DeviceIdType.MESH
F32, BF16 = jnp.float32, jnp.bfloat16
HEIGHT, WIDTH = 15, 15
GATHER_A = (0, 56)
REDUCE_A = (56, 0)
PITCH = 16


def split(value):
    high = value.astype(BF16)
    return high, (value - high.astype(F32)).astype(BF16)


def dot_nt(a, b):
    return lax.dot_general(a, b, (((1,), (1,)), ((), ())), preferred_element_type=F32)


def dot_nn(a, b):
    return lax.dot_general(a, b, (((1,), (0,)), ((), ())), preferred_element_type=F32)


def kernel(
    sections,
    replicas,
    act_in,
    act_mid,
    relu_mask,
    arriving,
    loss_grad,
    w_first,
    w_second,
    data_grad,
    first_grad,
    second_grad,
    raw_acts,
    raw_mask,
    raw_up,
    flat,
    act_t,
    rows_hi,
    rows_lo,
    cols_hi,
    cols_lo,
    weights,
    w_hi,
    w_lo,
    total,
    passed,
    above,
    grads,
    pair_in,
    ring_in,
    cross_b_in,
    cross_a_in,
    load_sem,
    own_sem,
    gather_send,
    gather_ring,
    gather_cross,
    gather_pair,
    shift_sem,
    reduce_send,
    reduce_pair,
    reduce_ring,
    reduce_cross_b,
    reduce_cross_a,
):
    ny = replicas // 4
    half = ny // 2
    shard, chans = w_first.shape[1:]
    size = HEIGHT * WIDTH
    rows = HEIGHT * PITCH
    taps = 7
    sec = lax.axis_index("section")
    dp = lax.axis_index("dp")
    x, y, c = dp // (2 * ny), (dp // 2) % ny, dp % 2

    def device(xr, rel, other):
        xx = 1 - x if xr else x
        cc = 1 - c if other else c
        return xx * (2 * ny) + lax.rem(y + rel + ny, ny) * 2 + cc

    def block(xr, rel, other=False, low=0, count=shard):
        return pl.ds(pl.multiple_of(device(xr, rel, other) * shard + low, 8), count)

    def slot(xr, rel):
        return xr * ny + rel % ny

    pair = {"dp": device(0, 0, True)}
    cross = {"dp": device(1, 0, False)}
    ahead = {1: {"dp": device(0, 1, False)}, -1: {"dp": device(0, -1, False)}}
    prev_section = {"section": lax.rem(sec + sections - 1, sections)}
    next_section = {"section": lax.rem(sec + 1, sections)}

    barrier = pltpu.get_barrier_semaphore()
    friends = (pair, cross, ahead[1], ahead[-1], prev_section, next_section)
    for friend in friends:
        pl.semaphore_signal(barrier, inc=1, device_id=friend, device_id_type=MESH)

    sources = (arriving, act_mid, act_in, relu_mask, loss_grad)
    targets = (raw_up.at[0], raw_acts.at[0], raw_acts.at[1], raw_mask, raw_up.at[1])
    loads = [
        pltpu.make_async_copy(s, d, load_sem.at[i])
        for i, (s, d) in enumerate(zip(sources, targets))
    ]
    for copy in loads:
        copy.start()
    shards = (w_second.at[0], w_first.at[0])
    own = [
        pltpu.make_async_copy(shards[w], weights.at[w, block(0, 0)], own_sem.at[w])
        for w in range(2)
    ]
    for copy in own:
        copy.start()

    def copy_to(src, dst, send_sem, recv_sem, to):
        return pltpu.make_async_remote_copy(
            src_ref=src,
            dst_ref=dst,
            send_sem=send_sem,
            recv_sem=recv_sem,
            device_id=to,
            device_id_type=MESH,
        )

    def allowed(w, way, xr, hop, last):
        return hop != last or (xr == 0) == ((way == 1) == (w == 0))

    def span(w, xr, first=GATHER_A):
        return (0, first[w]) if xr else (0, shard)

    def rest(w, first):
        return first[w], shard - first[w]

    def gather_ring_copy(w, way, xr, hop):
        at = block(xr, -way * hop, False, *span(w, xr))
        here = weights.at[w, at]
        sem = gather_ring.at[w, slot(xr, -way * hop)]
        return copy_to(here, here, gather_send.at[w], sem, ahead[way])

    def gather_on(w, way, xr, hop, src=None):
        if span(w, xr)[1] == 0:
            return
        here = weights.at[w, block(xr, -way * (hop - 1), False, *span(w, xr))]
        sem = gather_ring.at[w, slot(xr, -way * hop)]
        copy_to(here if src is None else src, here, gather_send.at[w], sem, ahead[way]).start()

    def gather_cross_copy(w, rel, sending, src=None):
        low, count = (0, shard) if rel == 0 else rest(w, GATHER_A)
        here = weights.at[w, block(0 if sending else 1, rel, False, low, count)]
        sem = gather_cross.at[w, rel % ny]
        return copy_to(here if src is None else src, here, gather_send.at[w], sem, cross)

    def gather_pair_copy(w, xr, rel, piece, sending, src=None):
        low, count = rest(w, GATHER_A) if piece else (0, shard)
        if piece == 0 and xr == 1 and rel % ny:
            count = GATHER_A[w]
        here = weights.at[w, block(xr, rel, not sending, low, count)]
        sem = gather_pair.at[w, slot(xr, rel), piece]
        return copy_to(here if src is None else src, here, gather_send.at[w], sem, pair)

    def gather_start(w):
        src = shards[w]
        gather_on(w, 1, 0, 1, src)
        gather_on(w, -1, 0, 1, src)
        gather_cross_copy(w, 0, True, src).start()
        gather_pair_copy(w, 0, 0, 0, True, src).start()

    def ring_arrival(w, way, xr, hop):
        if span(w, xr)[1] == 0:
            return
        gather_ring_copy(w, way, xr, hop).wait_recv()
        if hop < half and allowed(w, way, xr, hop + 1, half):
            gather_on(w, way, xr, hop + 1)
        if xr == 0 and GATHER_A[w] < shard:
            gather_cross_copy(w, -way * hop, True).start()
        gather_pair_copy(w, xr, -way * hop, 0, True).start()

    def cross_arrival(w, rel):
        if rel and GATHER_A[w] == shard:
            return
        gather_cross_copy(w, rel, False).wait_recv()
        if rel == 0:
            gather_on(w, 1, 1, 1)
            gather_on(w, -1, 1, 1)
            gather_pair_copy(w, 1, 0, 0, True).start()
        else:
            gather_pair_copy(w, 1, rel, 1, True).start()

    def gather_hop(w, xr, hop):
        for way in (1, -1):
            if allowed(w, way, xr, hop, half):
                ring_arrival(w, way, xr, hop)

    def gather_cross_hop(w, dist):
        for rel in (dist,) if dist in (0, half) else (dist, -dist):
            cross_arrival(w, rel)

    def gather_pair_wait(w):
        own[w].wait()
        for rel in range(ny):
            for xr in (0, 1):
                if xr == 0 or rel == 0 or GATHER_A[w]:
                    gather_pair_copy(w, xr, rel, 0, False).wait_recv()
            if rel and GATHER_A[w] < shard:
                gather_pair_copy(w, 1, rel, 1, False).wait_recv()

    def round_weights(w):
        high, low = split(weights[w])
        w_hi[w] = high
        w_lo[w] = low

    top = 3 * PITCH

    def flatten(raw, start, to):
        zero = jnp.zeros((PITCH - WIDTH, chans), F32)
        for h in range(HEIGHT):
            line = raw[pl.ds(start + h * WIDTH, WIDTH), 0, :].astype(F32)
            flat[to, h * PITCH : (h + 1) * PITCH] = jnp.concatenate([line, zero], axis=0)

    def set_rows(t, value):
        high, low = split(value)
        rows_hi[t, top : top + rows] = high
        rows_lo[t, top : top + rows] = low

    def row_tap(t, k, count):
        at = slice((6 - k) * PITCH, (6 - k) * PITCH + count)
        return rows_hi[t, at], rows_lo[t, at]

    def transpose_acts(which, t):
        flatten(raw_acts.at[which], t * size, 0)
        high, low = split(flat[0].T)
        act_t[which, t, 0] = high
        act_t[which, t, 1] = low

    def project(lhs, w, first=0, last=7):
        for k in range(first, last):
            at = pl.ds(k * chans, chans)
            high, low = lhs(k)
            part = (
                dot_nt(high, w_hi[w, at]) + dot_nt(high, w_lo[w, at]) + dot_nt(low, w_hi[w, at])
            )
            if k == 0:
                total[...] = part
            else:
                total[...] += part

    def correlate(w, t, rhs):
        for k in range(taps):
            at = pl.ds(k * chans, chans)
            high, low = rhs(k)
            a_hi, a_lo = act_t[w, t, 0], act_t[w, t, 1]
            part = dot_nn(a_hi, high) + dot_nn(a_hi, low) + dot_nn(a_lo, high)
            if t == 0:
                grads[w, at] = part
            else:
                grads[w, at] += part

    def set_cols(t):
        pre = total[...] * flat[1 + t, 0:rows]
        column = lax.broadcasted_iota(jnp.int32, (rows, chans), 0) % PITCH
        for k in range(taps):
            by = k - 3
            moved = pre if by == 0 else pltpu.roll(pre, by % rows, 0)
            inside = (column >= by) & (column < PITCH + by)
            high, low = split(jnp.where(inside, moved, 0.0))
            cols_hi[k, 0:rows] = high
            cols_lo[k, 0:rows] = low

    def col_tap(count):
        return lambda k: (cols_hi[k, 0:count], cols_lo[k, 0:count])

    def give_map(t):
        for h in range(HEIGHT):
            line = total[h * PITCH : (h + 1) * PITCH]
            data_grad[pl.ds(t * size + h * WIDTH, WIDTH), 0, :] = line[0:WIDTH]

    def pair_copy(w, xr, rel):
        return copy_to(
            grads.at[w, block(xr, rel, True)],
            pair_in.at[w, slot(xr, rel)],
            reduce_send.at[w],
            reduce_pair.at[w, slot(xr, rel)],
            pair,
        )

    def ring_copy(w, way, xr, hop):
        rel = way * (half + 1 - hop)
        lane = 0 if way == 1 else 1
        low, count = span(w, xr, REDUCE_A)
        return copy_to(
            grads.at[w, block(xr, rel, False, low, count)],
            ring_in.at[w, lane, hop - 1, xr, pl.ds(low, count)],
            reduce_send.at[w],
            reduce_ring.at[w, lane, hop - 1, xr],
            ahead[way],
        )

    def cross_b_copy(w, rel):
        return copy_to(
            grads.at[w, block(1, rel, False, *rest(w, REDUCE_A))],
            cross_b_in.at[w, rel % ny, pl.ds(*rest(w, REDUCE_A))],
            reduce_send.at[w],
            reduce_cross_b.at[w, rel % ny],
            cross,
        )

    def cross_a_copy(w):
        return copy_to(
            grads.at[w, block(1, 0, False, 0, REDUCE_A[w])],
            cross_a_in.at[w, pl.ds(0, REDUCE_A[w])],
            reduce_send.at[w],
            reduce_cross_a.at[w],
            cross,
        )

    outward = [half]
    for dist in range(half - 1, 0, -1):
        outward += [dist, -dist]
    outward.append(0)

    def pair_start(w):
        for rel in outward:
            for xr in (1, 0):
                pair_copy(w, xr, rel).start()

    def cross_hop(w):
        for rel in outward:
            pair_copy(w, 1, rel).wait_recv()
            here = block(1, rel)
            grads[w, here] += pair_in[w, slot(1, rel)]
            if REDUCE_A[w] < shard:
                cross_b_copy(w, rel).start()

    def came(w, way, xr, hop):
        return hop >= 1 and allowed(w, way, xr, hop, 1) and span(w, xr, REDUCE_A)[1] > 0

    def lane_of(way):
        return 0 if way == 1 else 1

    def own_column(w, rel):
        pair_copy(w, 0, rel).wait_recv()
        here = block(0, rel)
        grads[w, here] += pair_in[w, slot(0, rel)]
        if REDUCE_A[w] < shard:
            cross_b_copy(w, rel).wait_recv()
            low, count = rest(w, REDUCE_A)
            here = block(0, rel, False, low, count)
            grads[w, here] += cross_b_in[w, rel % ny, low : low + count]

    def ring_hop(w, hop, columns=(1, 0)):
        for xr in columns:
            for way in (1, -1):
                if not came(w, way, xr, hop):
                    continue
                rel = way * (half + 1 - hop)
                if xr == 0:
                    own_column(w, rel)
                if came(w, way, xr, hop - 1):
                    ring_copy(w, way, xr, hop - 1).wait_recv()
                    low, count = span(w, xr, REDUCE_A)
                    here = block(xr, rel, False, low, count)
                    grads[w, here] += ring_in[w, lane_of(way), hop - 2, xr, low : low + count]
                ring_copy(w, way, xr, hop).start()

    def ring_end(w):
        for xr in (1, 0):
            low, count = span(w, xr, REDUCE_A)
            if count == 0:
                continue
            here = block(xr, 0, False, low, count)
            if xr == 0:
                own_column(w, 0)
            for way in (1, -1):
                ring_copy(w, way, xr, half).wait_recv()
            grads[w, here] += (
                ring_in[w, 0, half - 1, xr, low : low + count]
                + ring_in[w, 1, half - 1, xr, low : low + count]
            )
            if xr == 1:
                cross_a_copy(w).start()

    def give_grad(w):
        scale = 1.0 / (2 * replicas)
        low, count = rest(w, REDUCE_A)
        grad_out = (second_grad, first_grad)[w]
        if low:
            cross_a_copy(w).wait_recv()
            first = grads[w, block(0, 0, False, 0, low)] + cross_a_in[w, 0:low]
            grad_out[0, 0:low] = first * scale
        if count:
            grad_out[0, low:shard] = grads[w, block(0, 0, False, low, count)] * scale

    rows_hi[...] = jnp.zeros_like(rows_hi)
    rows_lo[...] = jnp.zeros_like(rows_lo)
    cols_hi[:, rows:256] = jnp.zeros((taps, 256 - rows, chans), BF16)
    cols_lo[:, rows:256] = jnp.zeros((taps, 256 - rows, chans), BF16)
    flat[0, rows:256] = jnp.zeros((256 - rows, chans), F32)
    pl.semaphore_wait(barrier, len(friends))
    gather_start(0)
    loads[0].wait()
    flatten(raw_up.at[0], 0, 1)
    set_rows(0, flat[1, 0:rows])
    loads[1].wait()
    transpose_acts(0, 0)
    transpose_acts(0, 1)
    loads[2].wait()
    transpose_acts(1, 0)
    transpose_acts(1, 1)
    gather_start(1)
    loads[3].wait()
    for t in range(2):
        flatten(raw_mask, t * size, 1 + t)
    loads[4].wait()
    flatten(raw_up.at[1], 0, 3)
    gather_hop(0, 0, 1)
    gather_hop(1, 0, 1)
    gather_cross_hop(0, 0)
    gather_cross_hop(1, 0)
    for hop in range(2, half + 1):
        gather_hop(0, 0, hop)
        gather_hop(0, 1, hop - 1)
        if hop > 2:
            gather_hop(1, 1, hop - 2)
        else:
            correlate(0, 0, lambda k: row_tap(0, k, 256))
        gather_hop(1, 0, hop)
        if hop > 2:
            gather_cross_hop(0, hop - 2)
    gather_hop(0, 1, half)
    gather_hop(1, 1, half - 1)
    gather_cross_hop(0, half - 1)
    gather_cross_hop(0, half)
    for dist in range(1, half - 1):
        gather_cross_hop(1, dist)
    gather_hop(1, 1, half)
    gather_pair_wait(0)
    round_weights(0)
    project(lambda k: row_tap(0, k, rows), 0, 0, 3)
    gather_cross_hop(1, half - 1)
    project(lambda k: row_tap(0, k, rows), 0, 3, 7)
    gather_cross_hop(1, half)
    set_cols(0)
    gather_pair_wait(1)
    round_weights(1)
    project(col_tap(rows), 1)
    passed[...] = total[...]
    shift = copy_to(passed, above, shift_sem.at[0], shift_sem.at[1], prev_section)
    shift.start()
    give_map(0)
    correlate(1, 0, col_tap(256))
    shift.wait_recv()
    is_last = jnp.full((rows, chans), sec, jnp.int32) == sections - 1
    set_rows(1, jnp.where(is_last, flat[3, 0:rows], above[...]))
    correlate(0, 1, lambda k: row_tap(1, k, 256))
    pair_start(0)
    project(lambda k: row_tap(1, k, rows), 0)
    cross_hop(0)
    ring_hop(0, 1, (1,))
    set_cols(1)
    correlate(1, 1, col_tap(256))
    pair_start(1)
    ring_hop(0, 1, (0,))
    cross_hop(1)
    ring_hop(0, 2)
    ring_hop(1, 1)
    if half > 2:
        ring_hop(0, 3)
    project(col_tap(rows), 1, 0, 3)
    ring_hop(1, 2)
    if half > 2:
        ring_hop(0, 4)
    project(col_tap(rows), 1, 3, 7)
    give_map(1)
    if half > 2:
        ring_hop(1, 3)
    ring_end(0)
    if half > 2:
        ring_hop(1, 4)
    give_grad(0)
    ring_end(1)
    give_grad(1)

    shift.wait_send()
    sent = pl.ds(0, (4 * ny - 1) * shard)
    for w in range(2):
        for buffer, sem in ((weights, gather_send), (grads, reduce_send)):
            there = buffer.at[w, sent]
            copy_to(there, there, sem.at[w], sem.at[w], pair).wait_send()


def local(sections, replicas, *args):
    act_in, w_first = args[0], args[5]
    chans = act_in.shape[-1]
    shard = w_first.shape[1]
    all_rows = shard * replicas
    ny = replicas // 4
    rows, size = HEIGHT * PITCH, HEIGHT * WIDTH
    dma = pltpu.SemaphoreType.DMA
    anywhere = pl.BlockSpec(memory_space=pl.ANY)
    scratch = [
        pltpu.VMEM((2, 2 * size, 1, chans), F32),
        pltpu.VMEM((2 * size, 1, chans), jnp.int32),
        pltpu.VMEM((2, size, 1, chans), F32),
        pltpu.VMEM((4, 256, chans), F32),
        pltpu.VMEM((2, 2, 2, chans, 256), BF16),
        pltpu.VMEM((2, 6 * PITCH + 256, chans), BF16),
        pltpu.VMEM((2, 6 * PITCH + 256, chans), BF16),
        pltpu.VMEM((7, 256, chans), BF16),
        pltpu.VMEM((7, 256, chans), BF16),
        pltpu.VMEM((2, all_rows, chans), F32),
        pltpu.VMEM((2, all_rows, chans), BF16),
        pltpu.VMEM((2, all_rows, chans), BF16),
        pltpu.VMEM((rows, chans), F32),
        pltpu.VMEM((rows, chans), F32),
        pltpu.VMEM((rows, chans), F32),
        pltpu.VMEM((2, all_rows, chans), F32),
        pltpu.VMEM((2, 2 * ny, shard, chans), F32),
        pltpu.VMEM((2, 2, ny // 2, 2, shard, chans), F32),
        pltpu.VMEM((2, ny, shard, chans), F32),
        pltpu.VMEM((2, shard, chans), F32),
        dma((5,)),
        dma((2,)),
        dma((2,)),
        dma((2, 2 * ny)),
        dma((2, ny)),
        dma((2, 2 * ny, 2)),
        dma((2,)),
        dma((2,)),
        dma((2, 2 * ny)),
        dma((2, 2, ny // 2, 2)),
        dma((2, ny)),
        dma((2,)),
    ]
    maps, first, second = pl.pallas_call(
        functools.partial(kernel, sections, replicas),
        out_shape=(
            pltpu.VMEM((2 * size, 1, chans), F32),
            pltpu.VMEM(w_first.shape, F32),
            pltpu.VMEM(w_first.shape, F32),
        ),
        in_specs=[anywhere] * 7,
        out_specs=(pl.BlockSpec(memory_space=pltpu.VMEM),) * 3,
        scratch_shapes=scratch,
        compiler_params=pltpu.CompilerParams(collective_id=0, has_side_effects=True),
    )(*(a.reshape(-1, 1, chans) for a in args[:5]), *args[5:])
    return maps.reshape(act_in.shape), first, second


def solution(mesh):
    return jax.shard_map(
        functools.partial(local, mesh.shape["section"], mesh.shape["dp"]),
        mesh=mesh,
        in_specs=(
            P("section", None, "dp", None, None, None),
            P("section", None, "dp", None, None, None),
            P("section", None, "dp", None, None, None),
            P("section", "dp", None, None, None),
            P(None, "dp", None, None, None),
            P("section", "dp", None),
            P("section", "dp", None),
        ),
        out_specs=(
            P("section", None, "dp", None, None, None),
            P("section", "dp", None),
            P("section", "dp", None),
        ),
        check_vma=False,
    )
```

```python
import functools

import jax
import jax.numpy as jnp
from jax import lax
from jax.experimental import pallas as pl
from jax.experimental.pallas import tpu as pltpu
from jax.sharding import PartitionSpec as P

MESH = pl.DeviceIdType.MESH
F32, BF16 = jnp.float32, jnp.bfloat16
HEIGHT, WIDTH = 15, 15
GATHER_A = (0, 56)
REDUCE_A = (56, 0)
PIECES = ((0, 56),), ((0, 32), (32, 24))
PITCH = 16


def split(value):
    high = value.astype(BF16)
    return high, (value - high.astype(F32)).astype(BF16)


def dot_nt(a, b):
    return lax.dot_general(a, b, (((1,), (1,)), ((), ())), preferred_element_type=F32)


def dot_nn(a, b):
    return lax.dot_general(a, b, (((1,), (0,)), ((), ())), preferred_element_type=F32)


def kernel(
    sections,
    replicas,
    act_in,
    act_mid,
    relu_mask,
    arriving,
    loss_grad,
    w_first,
    w_second,
    data_grad,
    both_grads,
    raw_acts,
    raw_mask,
    raw_up,
    flat,
    act_t,
    rows_hi,
    rows_lo,
    cols_hi,
    cols_lo,
    weights,
    w_hi,
    w_lo,
    total,
    passed,
    above,
    grads,
    pair_in,
    ring_in,
    cross_b_in,
    cross_a_in,
    load_sem,
    own_sem,
    gather_send,
    gather_ring,
    gather_cross,
    gather_pair,
    shift_sem,
    reduce_send,
    reduce_pair,
    reduce_ring,
    reduce_cross_b,
    reduce_cross_a,
):
    ny = replicas // 4
    half = ny // 2
    shard, chans = w_first.shape[1:]
    size = HEIGHT * WIDTH
    rows = HEIGHT * PITCH
    taps = 7
    sec = lax.axis_index("section")
    dp = lax.axis_index("dp")
    x, y, c = dp // (2 * ny), (dp // 2) % ny, dp % 2

    def device(xr, rel, other):
        xx = 1 - x if xr else x
        cc = 1 - c if other else c
        return xx * (2 * ny) + lax.rem(y + rel + ny, ny) * 2 + cc

    def block(xr, rel, other=False, low=0, count=shard):
        return pl.ds(pl.multiple_of(device(xr, rel, other) * shard + low, 8), count)

    def slot(xr, rel):
        return xr * ny + rel % ny

    pair = {"dp": device(0, 0, True)}
    cross = {"dp": device(1, 0, False)}
    ahead = {1: {"dp": device(0, 1, False)}, -1: {"dp": device(0, -1, False)}}
    prev_section = {"section": lax.rem(sec + sections - 1, sections)}
    next_section = {"section": lax.rem(sec + 1, sections)}

    barrier = pltpu.get_barrier_semaphore()
    friends = (pair, cross, ahead[1], ahead[-1], prev_section, next_section)
    for friend in friends:
        pl.semaphore_signal(barrier, inc=1, device_id=friend, device_id_type=MESH)

    sources = (arriving, act_mid, act_in, relu_mask, loss_grad)
    targets = (raw_up.at[0], raw_acts.at[0], raw_acts.at[1], raw_mask, raw_up.at[1])
    loads = [
        pltpu.make_async_copy(s, d, load_sem.at[i])
        for i, (s, d) in enumerate(zip(sources, targets))
    ]
    for copy in loads:
        copy.start()
    shards = (w_second.at[0], w_first.at[0])
    own = [
        pltpu.make_async_copy(shards[w], weights.at[w, block(0, 0)], own_sem.at[w])
        for w in range(2)
    ]
    for copy in own:
        copy.start()

    def copy_to(src, dst, send_sem, recv_sem, to):
        return pltpu.make_async_remote_copy(
            src_ref=src,
            dst_ref=dst,
            send_sem=send_sem,
            recv_sem=recv_sem,
            device_id=to,
            device_id_type=MESH,
        )

    def allowed(w, way, xr, hop, last):
        return hop != last or (xr == 0) == ((way == 1) == (w == 0))

    def span(w, xr, first=GATHER_A):
        return (0, first[w]) if xr else (0, shard)

    def rest(w, first):
        return first[w], shard - first[w]

    def gather_ring_copy(w, way, xr, hop):
        at = block(xr, -way * hop, False, *span(w, xr))
        here = weights.at[w, at]
        sem = gather_ring.at[w, slot(xr, -way * hop)]
        return copy_to(here, here, gather_send.at[w], sem, ahead[way])

    def gather_on(w, way, xr, hop, src=None):
        if span(w, xr)[1] == 0:
            return
        here = weights.at[w, block(xr, -way * (hop - 1), False, *span(w, xr))]
        sem = gather_ring.at[w, slot(xr, -way * hop)]
        copy_to(here if src is None else src, here, gather_send.at[w], sem, ahead[way]).start()

    def gather_cross_copy(w, rel, sending, src=None):
        low, count = (0, shard) if rel == 0 else rest(w, GATHER_A)
        here = weights.at[w, block(0 if sending else 1, rel, False, low, count)]
        sem = gather_cross.at[w, rel % ny]
        return copy_to(here if src is None else src, here, gather_send.at[w], sem, cross)

    def gather_pair_copy(w, xr, rel, piece, sending, src=None):
        low, count = rest(w, GATHER_A) if piece else (0, shard)
        if piece == 0 and xr == 1 and rel % ny:
            count = GATHER_A[w]
        here = weights.at[w, block(xr, rel, not sending, low, count)]
        sem = gather_pair.at[w, slot(xr, rel), piece]
        return copy_to(here if src is None else src, here, gather_send.at[w], sem, pair)

    def gather_start(w):
        src = shards[w]
        gather_on(w, 1, 0, 1, src)
        gather_on(w, -1, 0, 1, src)
        gather_cross_copy(w, 0, True, src).start()
        gather_pair_copy(w, 0, 0, 0, True, src).start()

    def ring_arrival(w, way, xr, hop):
        if span(w, xr)[1] == 0:
            return
        gather_ring_copy(w, way, xr, hop).wait_recv()
        if hop < half and allowed(w, way, xr, hop + 1, half):
            gather_on(w, way, xr, hop + 1)
        if xr == 0 and GATHER_A[w] < shard:
            gather_cross_copy(w, -way * hop, True).start()
        gather_pair_copy(w, xr, -way * hop, 0, True).start()

    def cross_arrival(w, rel):
        if rel and GATHER_A[w] == shard:
            return
        gather_cross_copy(w, rel, False).wait_recv()
        if rel == 0:
            gather_on(w, 1, 1, 1)
            gather_on(w, -1, 1, 1)
            gather_pair_copy(w, 1, 0, 0, True).start()
        else:
            gather_pair_copy(w, 1, rel, 1, True).start()

    def gather_hop(w, xr, hop):
        for way in (1, -1):
            if allowed(w, way, xr, hop, half):
                ring_arrival(w, way, xr, hop)

    def gather_cross_hop(w, dist):
        for rel in (dist,) if dist in (0, half) else (dist, -dist):
            cross_arrival(w, rel)

    def gather_pair_wait(w):
        own[w].wait()
        for rel in range(ny):
            for xr in (0, 1):
                if xr == 0 or rel == 0 or GATHER_A[w]:
                    gather_pair_copy(w, xr, rel, 0, False).wait_recv()
            if rel and GATHER_A[w] < shard:
                gather_pair_copy(w, 1, rel, 1, False).wait_recv()

    def round_weights(w):
        high, low = split(weights[w])
        w_hi[w] = high
        w_lo[w] = low

    top = 3 * PITCH

    def flatten(raw, start, to):
        zero = jnp.zeros((PITCH - WIDTH, chans), F32)
        for h in range(HEIGHT):
            line = raw[pl.ds(start + h * WIDTH, WIDTH), 0, :].astype(F32)
            flat[to, h * PITCH : (h + 1) * PITCH] = jnp.concatenate([line, zero], axis=0)

    def set_rows(t, value):
        high, low = split(value)
        rows_hi[t, top : top + rows] = high
        rows_lo[t, top : top + rows] = low

    def row_tap(t, k, count):
        at = slice((6 - k) * PITCH, (6 - k) * PITCH + count)
        return rows_hi[t, at], rows_lo[t, at]

    def transpose_acts(which, t):
        flatten(raw_acts.at[which], t * size, 0)
        high, low = split(flat[0].T)
        act_t[which, t, 0] = high
        act_t[which, t, 1] = low

    def project(lhs, w, first=0, last=7):
        for k in range(first, last):
            at = pl.ds(k * chans, chans)
            high, low = lhs(k)
            part = (
                dot_nt(high, w_hi[w, at]) + dot_nt(high, w_lo[w, at]) + dot_nt(low, w_hi[w, at])
            )
            if k == 0:
                total[...] = part
            else:
                total[...] += part

    def correlate(w, t, rhs):
        for k in range(taps):
            at = pl.ds(k * chans, chans)
            high, low = rhs(k)
            a_hi, a_lo = act_t[w, t, 0], act_t[w, t, 1]
            part = dot_nn(a_hi, high) + dot_nn(a_hi, low) + dot_nn(a_lo, high)
            if t == 0:
                grads[w, at] = part
            else:
                grads[w, at] += part

    def set_cols(t):
        pre = total[...] * flat[1 + t, 0:rows]
        column = lax.broadcasted_iota(jnp.int32, (rows, chans), 0) % PITCH
        for k in range(taps):
            by = k - 3
            moved = pre if by == 0 else pltpu.roll(pre, by % rows, 0)
            inside = (column >= by) & (column < PITCH + by)
            high, low = split(jnp.where(inside, moved, 0.0))
            cols_hi[k, 0:rows] = high
            cols_lo[k, 0:rows] = low

    def col_tap(count):
        return lambda k: (cols_hi[k, 0:count], cols_lo[k, 0:count])

    def give_map(t):
        for h in range(HEIGHT):
            line = total[h * PITCH : (h + 1) * PITCH]
            data_grad[pl.ds(t * size + h * WIDTH, WIDTH), 0, :] = line[0:WIDTH]

    def pair_copy(w, xr, rel):
        return copy_to(
            grads.at[w, block(xr, rel, True)],
            pair_in.at[w, slot(xr, rel)],
            reduce_send.at[w],
            reduce_pair.at[w, slot(xr, rel)],
            pair,
        )

    def piece(w, xr, part, first=REDUCE_A):
        low, count = PIECES[w][part]
        return low, min(low + count, span(w, xr, first)[1]) - low

    def parts(w, xr):
        return [p for p in range(len(PIECES[w])) if piece(w, xr, p)[1] > 0]

    def ring_copy(w, way, xr, hop, part):
        rel = way * (half + 1 - hop)
        lane = 0 if way == 1 else 1
        low, count = piece(w, xr, part)
        return copy_to(
            grads.at[w, block(xr, rel, False, low, count)],
            ring_in.at[w, lane, hop - 1, xr, pl.ds(low, count)],
            reduce_send.at[w],
            reduce_ring.at[w, lane, hop - 1, xr, part],
            ahead[way],
        )

    def b_piece(w, part):
        low, count = PIECES[w][part]
        start = max(low, REDUCE_A[w])
        return start, low + count - start

    def cross_b_copy(w, rel, part):
        low, count = b_piece(w, part)
        return copy_to(
            grads.at[w, block(1, rel, False, low, count)],
            cross_b_in.at[w, rel % ny, pl.ds(low, count)],
            reduce_send.at[w],
            reduce_cross_b.at[w, rel % ny, part],
            cross,
        )

    def cross_a_copy(w):
        return copy_to(
            grads.at[w, block(1, 0, False, 0, REDUCE_A[w])],
            cross_a_in.at[w, pl.ds(0, REDUCE_A[w])],
            reduce_send.at[w],
            reduce_cross_a.at[w],
            cross,
        )

    outward = [half]
    for dist in range(half - 1, 0, -1):
        outward += [dist, -dist]
    outward.append(0)

    def pair_start(w):
        for rel in outward:
            for xr in (1, 0):
                pair_copy(w, xr, rel).start()

    def cross_hop(w, rels=outward):
        for rel in rels:
            pair_copy(w, 1, rel).wait_recv()
            here = block(1, rel)
            grads[w, here] += pair_in[w, slot(1, rel)]
            for part in range(len(PIECES[w])):
                if b_piece(w, part)[1] > 0:
                    cross_b_copy(w, rel, part).start()

    def came(w, way, xr, hop):
        return hop >= 1 and allowed(w, way, xr, hop, 1) and span(w, xr, REDUCE_A)[1] > 0

    def lane_of(way):
        return 0 if way == 1 else 1

    def own_column(w, rel, part):
        if part == 0:
            pair_copy(w, 0, rel).wait_recv()
            here = block(0, rel)
            grads[w, here] += pair_in[w, slot(0, rel)]
        low, count = b_piece(w, part)
        if count > 0:
            cross_b_copy(w, rel, part).wait_recv()
            here = block(0, rel, False, low, count)
            grads[w, here] += cross_b_in[w, rel % ny, low : low + count]

    def ring_hop(w, hop):
        for xr in (1, 0):
            for part in parts(w, xr):
                for way in (1, -1):
                    if not came(w, way, xr, hop):
                        continue
                    rel = way * (half + 1 - hop)
                    if xr == 0:
                        own_column(w, rel, part)
                    if came(w, way, xr, hop - 1):
                        ring_copy(w, way, xr, hop - 1, part).wait_recv()
                        low, count = piece(w, xr, part)
                        here = block(xr, rel, False, low, count)
                        lane = lane_of(way)
                        grads[w, here] += ring_in[w, lane, hop - 2, xr, low : low + count]
                    ring_copy(w, way, xr, hop, part).start()

    def ring_end(w, columns=(1, 0)):
        for xr in columns:
            for part in parts(w, xr):
                low, count = piece(w, xr, part)
                here = block(xr, 0, False, low, count)
                if xr == 0:
                    own_column(w, 0, part)
                for way in (1, -1):
                    ring_copy(w, way, xr, half, part).wait_recv()
                grads[w, here] += (
                    ring_in[w, 0, half - 1, xr, low : low + count]
                    + ring_in[w, 1, half - 1, xr, low : low + count]
                )
            if xr == 1 and REDUCE_A[w]:
                cross_a_copy(w).start()

    def give_grad(w):
        low, count = rest(w, REDUCE_A)
        if low:
            cross_a_copy(w).wait_recv()
            first = grads[w, block(0, 0, False, 0, low)] + cross_a_in[w, 0:low]
            both_grads[w, 0:low] = first
        if count:
            both_grads[w, low:shard] = grads[w, block(0, 0, False, low, count)]

    pl.semaphore_wait(barrier, len(friends))
    gather_start(0)
    rows_hi[...] = jnp.zeros_like(rows_hi)
    rows_lo[...] = jnp.zeros_like(rows_lo)
    cols_hi[:, rows:256] = jnp.zeros((taps, 256 - rows, chans), BF16)
    cols_lo[:, rows:256] = jnp.zeros((taps, 256 - rows, chans), BF16)
    flat[0, rows:256] = jnp.zeros((256 - rows, chans), F32)
    loads[0].wait()
    flatten(raw_up.at[0], 0, 1)
    set_rows(0, flat[1, 0:rows])
    loads[1].wait()
    transpose_acts(0, 0)
    transpose_acts(0, 1)
    loads[2].wait()
    transpose_acts(1, 0)
    transpose_acts(1, 1)
    gather_start(1)
    loads[3].wait()
    for t in range(2):
        flatten(raw_mask, t * size, 1 + t)
    loads[4].wait()
    flatten(raw_up.at[1], 0, 3)
    gather_hop(0, 0, 1)
    gather_hop(1, 0, 1)
    gather_cross_hop(0, 0)
    gather_cross_hop(1, 0)
    for hop in range(2, half + 1):
        gather_hop(0, 0, hop)
        gather_hop(1, 0, hop)
        gather_hop(0, 1, hop - 1)
        gather_hop(1, 1, hop - 1)
        gather_cross_hop(0, hop - 1)
    gather_hop(0, 1, half)
    gather_cross_hop(0, half)
    gather_pair_wait(0)
    round_weights(0)
    project(lambda k: row_tap(0, k, rows), 0, 0, 2)
    gather_hop(1, 1, half)
    for dist in range(1, half + 1):
        gather_cross_hop(1, dist)
    project(lambda k: row_tap(0, k, rows), 0, 2, 7)
    set_cols(0)
    gather_pair_wait(1)
    round_weights(1)
    project(col_tap(rows), 1)
    passed[...] = total[...]
    shift = copy_to(passed, above, shift_sem.at[0], shift_sem.at[1], prev_section)
    shift.start()
    give_map(0)
    correlate(1, 0, col_tap(256))
    correlate(0, 0, lambda k: row_tap(0, k, 256))
    shift.wait_recv()
    is_last = jnp.full((rows, chans), sec, jnp.int32) == sections - 1
    set_rows(1, jnp.where(is_last, flat[3, 0:rows], above[...]))
    correlate(0, 1, lambda k: row_tap(1, k, 256))
    pair_start(0)
    project(lambda k: row_tap(1, k, rows), 0)
    cross_hop(0)
    ring_hop(0, 1)
    set_cols(1)
    correlate(1, 1, col_tap(256))
    pair_start(1)
    cross_hop(1, outward[:1])
    if half > 2:
        ring_hop(0, 2)
    cross_hop(1, outward[1:])
    ring_hop(1, 1)
    for hop in range(2, half):
        ring_hop(0, hop + 1)
        if hop == 2:
            project(col_tap(rows), 1, 0, 3)
        ring_hop(1, hop)
    if half == 2:
        project(col_tap(rows), 1, 0, 3)
        ring_hop(0, 2)
    project(col_tap(rows), 1, 3, 7)
    give_map(1)
    ring_end(0, (1,))
    ring_hop(1, half)
    ring_end(0, (0,))
    give_grad(0)
    ring_end(1)
    give_grad(1)

    shift.wait_send()
    sent = pl.ds(0, (4 * ny - 1) * shard)
    for w in range(2):
        for buffer, sem in ((weights, gather_send), (grads, reduce_send)):
            there = buffer.at[w, sent]
            copy_to(there, there, sem.at[w], sem.at[w], pair).wait_send()


def local(sections, replicas, *args):
    act_in, w_first = args[0], args[5]
    chans = act_in.shape[-1]
    shard = w_first.shape[1]
    all_rows = shard * replicas
    ny = replicas // 4
    rows, size = HEIGHT * PITCH, HEIGHT * WIDTH
    dma = pltpu.SemaphoreType.DMA
    anywhere = pl.BlockSpec(memory_space=pl.ANY)
    scratch = [
        pltpu.VMEM((2, 2 * size, 1, chans), F32),
        pltpu.VMEM((2 * size, 1, chans), jnp.int32),
        pltpu.VMEM((2, size, 1, chans), F32),
        pltpu.VMEM((4, 256, chans), F32),
        pltpu.VMEM((2, 2, 2, chans, 256), BF16),
        pltpu.VMEM((2, 6 * PITCH + 256, chans), BF16),
        pltpu.VMEM((2, 6 * PITCH + 256, chans), BF16),
        pltpu.VMEM((7, 256, chans), BF16),
        pltpu.VMEM((7, 256, chans), BF16),
        pltpu.VMEM((2, all_rows, chans), F32),
        pltpu.VMEM((2, all_rows, chans), BF16),
        pltpu.VMEM((2, all_rows, chans), BF16),
        pltpu.VMEM((rows, chans), F32),
        pltpu.VMEM((rows, chans), F32),
        pltpu.VMEM((rows, chans), F32),
        pltpu.VMEM((2, all_rows, chans), F32),
        pltpu.VMEM((2, 2 * ny, shard, chans), F32),
        pltpu.VMEM((2, 2, ny // 2, 2, shard, chans), F32),
        pltpu.VMEM((2, ny, shard, chans), F32),
        pltpu.VMEM((2, shard, chans), F32),
        dma((5,)),
        dma((2,)),
        dma((2,)),
        dma((2, 2 * ny)),
        dma((2, ny)),
        dma((2, 2 * ny, 2)),
        dma((2,)),
        dma((2,)),
        dma((2, 2 * ny)),
        dma((2, 2, ny // 2, 2, 2)),
        dma((2, ny, 2)),
        dma((2,)),
    ]
    maps, both = pl.pallas_call(
        functools.partial(kernel, sections, replicas),
        out_shape=(
            pltpu.VMEM((2 * size, 1, chans), F32),
            pltpu.VMEM((2, shard, chans), F32),
        ),
        in_specs=[anywhere] * 7,
        out_specs=(pl.BlockSpec(memory_space=pltpu.VMEM),) * 2,
        scratch_shapes=scratch,
        compiler_params=pltpu.CompilerParams(collective_id=0, has_side_effects=True),
    )(*(a.reshape(-1, 1, chans) for a in args[:5]), *args[5:])
    both = both * (1.0 / (2 * replicas))
    return maps.reshape(act_in.shape), both[1:], both[:1]


def solution(mesh):
    return jax.shard_map(
        functools.partial(local, mesh.shape["section"], mesh.shape["dp"]),
        mesh=mesh,
        in_specs=(
            P("section", None, "dp", None, None, None),
            P("section", None, "dp", None, None, None),
            P("section", None, "dp", None, None, None),
            P("section", "dp", None, None, None),
            P(None, "dp", None, None, None),
            P("section", "dp", None),
            P("section", "dp", None),
        ),
        out_specs=(
            P("section", None, "dp", None, None, None),
            P("section", "dp", None),
            P("section", "dp", None),
        ),
        check_vma=False,
    )
```
